32 devices in a mesh: groups: 2 (over x), qrow: 4 (over y, core), kcol: 4 (over z).
Axes of the slice: x: 2, y: 2, z: 4, core: 2. Of those that a mesh axis runs over, the one named last changes fastest.
Arguments:
- queries: bfloat16 [8192, 512], P(('groups', 'qrow', 'kcol')), parts along dimension 0, may hold values from -6 to 6
- keys: bfloat16 [8192, 128], P(('groups', 'kcol', 'qrow')), parts along dimension 0, may hold values from -6 to 6
- values: bfloat16 [8192, 128], P(('groups', 'kcol', 'qrow')), parts along dimension 0, may hold values from -6 to 6
- out_grad: bfloat16 [8192, 512], P(('groups', 'qrow', 'kcol')), parts along dimension 0, may hold values from -6 to 6
- pattern: int32 [64, 10], P('groups'), parts along dimension 0, may hold values from 0 to 31, as said below
Outputs:
- attended: bfloat16 [8192, 512], P(('groups', 'qrow', 'kcol')), parts along dimension 0
- query_grad: bfloat16 [8192, 512], P(('groups', 'qrow', 'kcol')), parts along dimension 0
- key_grad: bfloat16 [8192, 128], P(('groups', 'kcol', 'qrow')), parts along dimension 0
- value_grad: bfloat16 [8192, 128], P(('groups', 'kcol', 'qrow')), parts along dimension 0
The draws below stay inside these ranges and needn't reach their ends.
There are 2 independent parts, one for each index of `groups`. The reference program is written for one: setup_inputs(seed, part) draws one part's arguments, and reference() takes and returns one part's arrays. A program takes and returns all parts, laid end to end along the dimension named above; each array names one. Nothing has to cross between parts.
Inputs may be any that keep to these rules, and one draw needn't show every extreme that they name: `pattern`: each row lists distinct key blocks, block b among them. Counting key blocks in aligned groups of 8, a row has at least one entry in every group, at most 4 in one group, and exactly 4 in the group that holds b.
All inputs are finite; a program needn't handle non-finite values.
Results may differ from the reference program's by a relative error of at most 0.038.
Values may be sent and summed in bfloat16 or wider, within the bound.
A program may use at most 128 MiB of HBM per device.

```python
import jax
import jax.numpy as jnp
from jax import lax

H = 4
HD = 128
BLK = 128
OTH = 2
TOKENS = 4096
NB = 32
KB = 8
CAP = 4
NNZ = 10


def background(key, shape):
    return jax.random.truncated_normal(key, -6.0, 6.0, shape)


def draw_queries(key, part):
    field = background(jax.random.fold_in(key, 1), (NB, BLK, H, HD))
    return field.reshape(TOKENS, H * HD).astype(jnp.bfloat16)


def draw_keys(key, part):
    field = background(jax.random.fold_in(key, 2), (NB, BLK, HD))
    return field.reshape(TOKENS, HD).astype(jnp.bfloat16)


def draw_pattern(key, part):
    row_ids = jnp.arange(NB, dtype=jnp.int32)
    home_group = row_ids // KB
    offset_in = row_ids % KB
    nearby = home_group[:, None] * KB + (offset_in[:, None] + jnp.arange(CAP, dtype=jnp.int32)[None, :] - CAP // 2) % KB
    spacing = KB // OTH
    pieces = [nearby]
    group_count = (NNZ - CAP) // OTH + 1
    for shift_by in range(1, group_count):
        target = (home_group + shift_by) % group_count
        phases = jax.random.randint(jax.random.fold_in(key, shift_by), (NB,), 0, spacing)
        spots = (offset_in[:, None] + phases[:, None] + jnp.arange(OTH, dtype=jnp.int32)[None, :] * spacing) % KB
        pieces.append(target[:, None] * KB + spots)
    listing = jnp.concatenate(pieces, axis=1)
    ranking = jax.random.randint(jax.random.fold_in(key, 999), (NB, NNZ), 0, 1000) * NNZ + jnp.arange(NNZ, dtype=jnp.int32)[None, :]
    ordering = jnp.argsort(ranking, axis=1)
    return jnp.take_along_axis(listing, ordering, axis=1).astype(jnp.int32)


def shard_levels(stream_key, extent, cuts, smallest, high):
    factor_of, own = 1.0, jax.random.fold_in(stream_key, 6)
    for axis_at, parts in cuts:
        heights = jnp.exp(jax.random.uniform(jax.random.fold_in(own, axis_at), (parts,), jnp.float32, smallest / len(cuts), high / len(cuts)))
        factor_of = factor_of * jnp.repeat(heights, extent[axis_at] // parts).reshape([-1 if axis == axis_at else 1 for axis in range(len(extent))])
    return factor_of


def normal_values(rng, dims, scale, limit, shards=(), kind=jnp.bfloat16):
    drawn = scale * jax.random.normal(rng, dims, jnp.float32)
    if shards:
        drawn = drawn * shard_levels(rng, dims, shards, -0.22, 0.18)
    return jnp.clip(drawn, -limit, limit).astype(kind)


def setup_inputs(seed: int = 0, part: int = 0) -> dict:
    key_list = jax.random.split(jax.random.key(seed), 6)
    part_splits = jax.random.split(jax.random.fold_in(key_list[5], part), 6)
    return {
        "queries": draw_queries(jax.random.fold_in(jax.random.fold_in(key_list[5], part), 71), part),
        "keys": draw_keys(jax.random.fold_in(jax.random.fold_in(key_list[5], part), 71), part),
        "values": normal_values(part_splits[2], (TOKENS, HD), 1.0, 6.0, ((0, 16),)),
        "out_grad": normal_values(part_splits[3], (TOKENS, H * HD), 1.0, 6.0, ((0, 16),)),
        "pattern": draw_pattern(jax.random.fold_in(jax.random.fold_in(key_list[5], part), 71), part),
    }


def reference(queries, keys, values, out_grad, pattern):
    scaling = HD ** -0.5
    k_tiles = keys.reshape(NB, BLK, HD)
    v_tiles = values.reshape(NB, BLK, HD)
    q_blocks = queries.reshape(NB, BLK, H, HD)
    g_blocks = out_grad.reshape(NB, BLK, H, HD)

    def block_scores(q_block, entries):
        k_slots = k_tiles[entries].reshape(NNZ * BLK, HD).astype(jnp.float32)
        scores = jnp.einsum("thd,sd->hts", q_block.astype(jnp.float32), k_slots) * scaling
        return scores, k_slots

    def forward(packed):
        q_block, g_block, entries = packed
        scores, k_slots = block_scores(q_block, entries)
        v_slots = v_tiles[entries].reshape(NNZ * BLK, HD).astype(jnp.float32)
        row_top = jnp.max(scores, axis=2)
        weights = jnp.exp(scores - row_top[:, :, None])
        totals = jnp.sum(weights, axis=2)
        weights_low = lax.optimization_barrier(weights.astype(jnp.bfloat16)).astype(jnp.float32)
        mixture = jnp.einsum("hts,sd->thd", weights_low, v_slots)
        attended = (mixture / jnp.transpose(totals)[:, :, None]).astype(jnp.bfloat16)
        log_sum = row_top + jnp.log(totals)
        delta = jnp.sum(g_block.astype(jnp.float32) * attended.astype(jnp.float32), axis=2)
        return attended, log_sum, delta

    attended, log_sums, deltas = lax.map(forward, (q_blocks, g_blocks, pattern))

    def backward(carried, packed):
        key_acc, value_acc = carried
        q_block, g_block, entries, log_sum, delta = packed
        scores, k_slots = block_scores(q_block, entries)
        v_slots = v_tiles[entries].reshape(NNZ * BLK, HD).astype(jnp.float32)
        prob_full = jnp.exp(scores - log_sum[:, :, None])
        prob_low = lax.optimization_barrier(prob_full.astype(jnp.bfloat16)).astype(jnp.float32)
        g_float = g_block.astype(jnp.float32)
        grad_prob = jnp.einsum("thd,sd->hts", g_float, v_slots)
        grad_score = prob_full * (grad_prob - jnp.transpose(delta)[:, :, None])
        grad_score = lax.optimization_barrier(grad_score.astype(jnp.bfloat16)).astype(jnp.float32)
        grad_query = jnp.einsum("hts,sd->thd", grad_score, k_slots) * scaling
        grad_key = jnp.einsum("hts,thd->sd", grad_score, q_block.astype(jnp.float32)) * scaling
        grad_value = jnp.einsum("hts,thd->sd", prob_low, g_float)
        key_acc = key_acc.at[entries].add(grad_key.reshape(NNZ, BLK, HD))
        value_acc = value_acc.at[entries].add(grad_value.reshape(NNZ, BLK, HD))
        return (key_acc, value_acc), grad_query.astype(jnp.bfloat16)

    empty_acc = jnp.zeros((NB, BLK, HD), jnp.float32)
    (key_acc, value_acc), grad_queries = lax.scan(
        backward, (empty_acc, empty_acc), (q_blocks, g_blocks, pattern, log_sums, deltas))
    return (attended.reshape(TOKENS, H * HD),
            grad_queries.reshape(TOKENS, H * HD),
            key_acc.reshape(TOKENS, HD).astype(jnp.bfloat16),
            value_acc.reshape(TOKENS, HD).astype(jnp.bfloat16))
```

```python
import functools
import math

import jax
import jax.numpy as jnp
from jax import lax
from jax.experimental import pallas as pl
from jax.experimental.pallas import tpu as pltpu
from jax.sharding import PartitionSpec as P

H = 4
HD = 128
BLK = 128
MESH = pl.DeviceIdType.MESH
F32 = jnp.float32
BF16 = jnp.bfloat16


def dot(a, b):
    return jnp.dot(a, b, preferred_element_type=F32)


def dot_t(a, b):
    return lax.dot_general(a, b, (((0,), (0,)), ((), ())), preferred_element_type=F32)


def kernel(
    nq, nk, nnz, q_ref, g_ref, k_ref, v_ref, pat_ref, o_ref, dq_ref, dk_ref, dv_ref,
    kv, core_in, y_in, z_in, slots, s_scr, qs, gs, qt, gt, kc_scr, vc_scr, inv,
    ag_send, ag_recv, core_send, core_recv, y_send, y_recv, z_send, z_recv,
):
    ny = nq // 2
    qb = q_ref.shape[0] // BLK
    kb = k_ref.shape[0] // BLK
    key_blocks = nq * nk * kb
    chunk = 2 if nnz % 2 == 0 else 1
    scaling = HD ** (-0.5)
    r = lax.axis_index("qrow")
    c = lax.axis_index("kcol")
    y, core = r // 2, r % 2
    other = 1 - core

    def shard(c_at, y_at, core_at):
        return c_at * nq + y_at * 2 + core_at

    def zed(d):
        return (c + d) % nk

    def why(e):
        return (y + e) % ny

    def at(c_to, y_to, core_to):
        return {"qrow": y_to * 2 + core_to, "kcol": c_to}

    def remote(src, dst, send, recv, where):
        return pltpu.make_async_remote_copy(
            src_ref=src, dst_ref=dst, send_sem=send, recv_sem=recv,
            device_id=where, device_id_type=MESH,
        )

    core_peer = at(c, y, other)

    barrier = pltpu.get_barrier_semaphore()
    for d in range(1, nk):
        pl.semaphore_signal(barrier, inc=1, device_id=at(zed(d), y, core), device_id_type=MESH)
    for e in range(1, ny):
        pl.semaphore_signal(barrier, inc=1, device_id=at(c, why(e), core), device_id_type=MESH)
    pl.semaphore_signal(barrier, inc=1, device_id=core_peer, device_id_type=MESH)

    own = shard(c, y, core)
    kv[own, 0] = k_ref[...].reshape(kb, BLK, HD)
    kv[own, 1] = v_ref[...].reshape(kb, BLK, HD)
    pl.semaphore_wait(barrier, nk - 1 + ny - 1 + 1)

    z_sends = nk - 1
    y_sends = nk * (ny - 1)

    def gather(slot, s, where):
        return remote(kv.at[s], kv.at[s], ag_send.at[slot], ag_recv.at[s], where)

    def arrived(s):
        gather(0, s, core_peer).wait_recv()

    for d in range(1, nk):
        gather(d - 1, own, at(zed(d), y, core)).start()
    for e in range(1, ny):
        gather(z_sends + e - 1, own, at(c, why(e), core)).start()
    gather(z_sends + y_sends, own, core_peer).start()

    for b in range(qb):
        for h in range(H):
            q_h = q_ref[b * BLK : (b + 1) * BLK, h * HD : (h + 1) * HD]
            g_h = g_ref[b * BLK : (b + 1) * BLK, h * HD : (h + 1) * HD]
            qs[b, h * BLK : (h + 1) * BLK, :] = q_h
            gs[b, h * BLK : (h + 1) * BLK, :] = g_h
            qt[b, :, h * BLK : (h + 1) * BLK] = q_h.T
            gt[b, :, h * BLK : (h + 1) * BLK] = g_h.T

    zero_slot = qb * nnz
    slots[0, zero_slot] = jnp.zeros((BLK, HD), F32)
    slots[1, zero_slot] = jnp.zeros((BLK, HD), F32)
    first_row = (r * nk + c) * qb

    for d in range(1, nk):
        s = shard(zed(nk - d), y, core)
        arrived(s)
        for e in range(1, ny):
            gather(z_sends + d * (ny - 1) + e - 1, s, at(c, why(e), core)).start()
        gather(z_sends + y_sends + d, s, core_peer).start()

    def invert(j, carry):
        for b in range(qb):
            found = jnp.int32(zero_slot)
            for n in range(nnz):
                found = jnp.where(pat_ref[first_row + b, n] == j, b * nnz + n, found)
            inv[b, j] = found
        return carry

    lax.fori_loop(0, key_blocks, invert, 0)

    def from_y(i, carry):
        e, d = i // nk + 1, i % nk
        s = shard(zed(nk - d), why(ny - e), core)
        arrived(s)
        gather(z_sends + y_sends + nk + i, s, core_peer).start()
        return carry

    lax.fori_loop(0, y_sends, from_y, 0)

    def from_core(i, carry):
        arrived(shard(i % nk, i // nk, other))
        return carry

    lax.fori_loop(0, nk * ny, from_core, 0)

    rows = chunk * BLK
    for b in range(qb):
        for n in range(nnz):
            j = pat_ref[first_row + b, n]
            kc_scr[b, n * BLK : (n + 1) * BLK, :] = kv[j // kb, 0, j % kb]
            vc_scr[b, n * BLK : (n + 1) * BLK, :] = kv[j // kb, 1, j % kb]
    for b in range(qb):
        top = None
        for n in range(0, nnz, chunk):
            part = slice(n * BLK, n * BLK + rows)
            scores = dot(kc_scr[b, part, :], qt[b])
            s_scr[b, part, :] = scores
            high = jnp.max(scores, axis=0, keepdims=True)
            top = high if top is None else jnp.maximum(top, high)
        total = jnp.zeros((1, H * BLK), F32)
        mix = jnp.zeros((HD, H * BLK), F32)
        for n in range(0, nnz, chunk):
            part = slice(n * BLK, n * BLK + rows)
            weights = jnp.exp2((s_scr[b, part, :] - top) * (scaling * math.log2(math.e)))
            s_scr[b, part, :] = weights
            total = total + jnp.sum(weights, axis=0, keepdims=True)
            mix = mix + dot_t(vc_scr[b, part, :], weights.astype(BF16))
        attended = (mix / total).astype(BF16)
        delta = jnp.sum(gt[b].astype(F32) * attended.astype(F32), axis=0, keepdims=True)
        share = 1.0 / total
        for h in range(H):
            o_ref[b * BLK : (b + 1) * BLK, h * HD : (h + 1) * HD] = attended[
                :, h * BLK : (h + 1) * BLK
            ].T
        grad_q = jnp.zeros((HD, H * BLK), F32)
        for n in range(0, nnz, chunk):
            part = slice(n * BLK, n * BLK + rows)
            grad_prob = dot(vc_scr[b, part, :], gt[b])
            prob = s_scr[b, part, :] * share
            grad_score = (prob * (grad_prob - delta)).astype(BF16)
            grad_v = dot(prob.astype(BF16), gs[b])
            grad_k = dot(grad_score, qs[b]) * scaling
            grad_q = grad_q + dot_t(kc_scr[b, part, :], grad_score)
            for i in range(chunk):
                slots[0, b * nnz + n + i] = grad_k[i * BLK : (i + 1) * BLK]
                slots[1, b * nnz + n + i] = grad_v[i * BLK : (i + 1) * BLK]
        grad_q = (grad_q * scaling).astype(BF16)
        for h in range(H):
            dq_ref[b * BLK : (b + 1) * BLK, h * HD : (h + 1) * HD] = grad_q[
                :, h * BLK : (h + 1) * BLK
            ].T

    def gathers_sent(i, carry):
        gather(i, own, core_peer).wait_send()
        return carry

    lax.fori_loop(0, z_sends + y_sends + nk * ny, gathers_sent, 0)

    def partial(s, which, half):
        j = s * kb + half
        value = slots[which, inv[0, j]]
        for b in range(1, qb):
            value = value + slots[which, inv[b, j]]
        return value

    def to_core(i, s):
        return remote(kv.at[s], core_in.at[i], core_send.at[i], core_recv.at[i], core_peer)

    def to_y(i, s, c_at, where, slot):
        return remote(kv.at[s], y_in.at[i], y_send.at[slot], y_recv.at[i], where)

    def to_z(i, s, where):
        return remote(kv.at[s], z_in.at[i], z_send.at[i], z_recv.at[i], where)

    def order(i):
        return zed((i % nk + 1) % nk), why((i // nk + 1) % ny)

    def core_step(i, carry):
        c_at, y_at = order(i)
        s = shard(c_at, y_at, other)
        for which in range(2):
            for half in range(kb):
                kv[s, which, half] = partial(s, which, half).astype(BF16)
        to_core(i, s).start()
        return carry

    lax.fori_loop(0, nk * ny, core_step, 0)

    def y_step(i, carry):
        c_at, y_at = order(i)
        s = shard(c_at, y_at, core)
        to_core(i, s).wait_recv()
        for which in range(2):
            for half in range(kb):
                value = partial(s, which, half) + core_in[i, which, half].astype(F32)
                kv[s, which, half] = value.astype(BF16)
        to_y(i, s, c_at, at(c, y_at, core), i).start()
        return carry

    lax.fori_loop(0, y_sends, y_step, 0)

    def summed(d, s, which, half):
        i = y_sends + (d + nk - 1) % nk
        value = partial(s, which, half) + core_in[i, which, half].astype(F32)
        for e in range(1, ny):
            value = value + y_in[(e - 1) * nk + (d + nk - 1) % nk, which, half].astype(F32)
        return value

    def landed(d, s):
        to_core(y_sends + (d + nk - 1) % nk, s).wait_recv()
        for e in range(1, ny):
            to_y((e - 1) * nk + (d + nk - 1) % nk, s, c, core_peer, 0).wait_recv()

    for d in range(1, nk):
        s = shard(zed(d), y, core)
        landed(d, s)
        for which in range(2):
            for half in range(kb):
                kv[s, which, half] = summed(d, s, which, half).astype(BF16)
        to_z(d - 1, s, at(zed(d), y, core)).start()
    landed(0, own)
    for d in range(1, nk):
        to_z(d - 1, own, core_peer).wait_recv()
    for which, out in ((0, dk_ref), (1, dv_ref)):
        for half in range(kb):
            value = summed(0, own, which, half)
            for d in range(1, nk):
                value = value + z_in[d - 1, which, half].astype(F32)
            out[half * BLK : (half + 1) * BLK, :] = value.astype(BF16)

    def core_sent(i, carry):
        to_core(i, own).wait_send()
        return carry

    def y_sent(i, carry):
        to_y(0, own, c, core_peer, i).wait_send()
        return carry

    lax.fori_loop(0, nk * ny, core_sent, 0)
    lax.fori_loop(0, y_sends, y_sent, 0)
    for d in range(1, nk):
        to_z(d - 1, own, core_peer).wait_send()


def body(nq, nk, queries, keys, values, out_grad, pattern):
    nnz = pattern.shape[1]
    ny = nq // 2
    qb = queries.shape[0] // BLK
    kb = keys.shape[0] // BLK
    shards = nq * nk
    block = (2, kb, BLK, HD)
    y_sends = nk * (ny - 1)
    dma = pltpu.SemaphoreType.DMA
    vmem = pl.BlockSpec(memory_space=pltpu.VMEM)
    return pl.pallas_call(
        functools.partial(kernel, nq, nk, nnz),
        out_shape=(
            jax.ShapeDtypeStruct(queries.shape, BF16),
            jax.ShapeDtypeStruct(queries.shape, BF16),
            jax.ShapeDtypeStruct(keys.shape, BF16),
            jax.ShapeDtypeStruct(keys.shape, BF16),
        ),
        in_specs=[vmem] * 4 + [pl.BlockSpec(memory_space=pltpu.SMEM)],
        out_specs=(vmem,) * 4,
        scratch_shapes=[
            pltpu.VMEM((shards,) + block, BF16),
            pltpu.VMEM((nk * ny,) + block, BF16),
            pltpu.VMEM((max(y_sends, 1),) + block, BF16),
            pltpu.VMEM((max(nk - 1, 1),) + block, BF16),
            pltpu.VMEM((2, qb * nnz + 1, BLK, HD), F32),
            pltpu.VMEM((qb, nnz * BLK, H * BLK), F32),
            pltpu.VMEM((qb, H * BLK, HD), BF16),
            pltpu.VMEM((qb, H * BLK, HD), BF16),
            pltpu.VMEM((qb, HD, H * BLK), BF16),
            pltpu.VMEM((qb, HD, H * BLK), BF16),
            pltpu.VMEM((qb, nnz * BLK, HD), BF16),
            pltpu.VMEM((qb, nnz * BLK, HD), BF16),
            pltpu.SMEM((qb, shards * kb), jnp.int32),
            dma((nk - 1 + y_sends + nk * ny,)),
            dma((shards,)),
            dma((nk * ny,)),
            dma((nk * ny,)),
            dma((max(y_sends, 1),)),
            dma((max(y_sends, 1),)),
            dma((max(nk - 1, 1),)),
            dma((max(nk - 1, 1),)),
        ],
        compiler_params=pltpu.CompilerParams(
            collective_id=0, has_side_effects=True, vmem_limit_bytes=58 * 1024 * 1024
        ),
    )(queries, out_grad, keys, values, pattern)


def solution(mesh):
    return jax.shard_map(
        functools.partial(body, mesh.shape["qrow"], mesh.shape["kcol"]),
        mesh=mesh,
        in_specs=(
            P(("groups", "qrow", "kcol"), None),
            P(("groups", "kcol", "qrow"), None),
            P(("groups", "kcol", "qrow"), None),
            P(("groups", "qrow", "kcol"), None),
            P("groups", None),
        ),
        out_specs=(
            P(("groups", "qrow", "kcol"), None),
            P(("groups", "qrow", "kcol"), None),
            P(("groups", "kcol", "qrow"), None),
            P(("groups", "kcol", "qrow"), None),
        ),
        check_vma=False,
    )
```

```python
import functools
import math

import jax
import jax.numpy as jnp
from jax import lax
from jax.experimental import pallas as pl
from jax.experimental.pallas import tpu as pltpu
from jax.sharding import PartitionSpec as P

H = 4
HD = 128
BLK = 128
MESH = pl.DeviceIdType.MESH
F32 = jnp.float32
BF16 = jnp.bfloat16


def dot(a, b):
    return jnp.dot(a, b, preferred_element_type=F32)


def dot_t(a, b):
    return lax.dot_general(a, b, (((0,), (0,)), ((), ())), preferred_element_type=F32)


def kernel(
    nq, nk, nnz, q_hbm, g_hbm, k_hbm, v_hbm, pat_ref, o_ref, dq_ref, dk_ref, dv_ref,
    k_all, v_all, core_in, y_in, z_in, slots, s_scr, q_ref, g_ref, qs, gs, qt, gt, kc_scr, vc_scr, inv,
    load_sem, ag_send, ag_recv, core_send, core_recv, y_send, y_recv, z_send, z_recv,
):
    ny = nq // 2
    qb = q_ref.shape[0] // BLK
    kb = k_hbm.shape[0]
    key_blocks = nq * nk * kb
    chunk = 2 if nnz % 2 == 0 else 1
    rows = chunk * BLK
    scaling = HD ** (-0.5)
    r = lax.axis_index("qrow")
    c = lax.axis_index("kcol")
    y, core = r // 2, r % 2
    other = 1 - core
    KEY, VALUE = 0, 1
    kv = (k_all, v_all)

    loads = [
        pltpu.make_async_copy(src, dst, load_sem.at[i])
        for i, (src, dst) in enumerate(
            (
                (k_hbm, k_all.at[pl.ds((c * nq + r) * kb, kb)]),
                (v_hbm, v_all.at[pl.ds((c * nq + r) * kb, kb)]),
                (q_hbm, q_ref),
                (g_hbm, g_ref),
            )
        )
    ]
    for load in loads:
        load.start()

    def shard(c_at, y_at, core_at):
        return c_at * nq + y_at * 2 + core_at

    def why(e):
        return (y + e) % ny

    def at(c_to, y_to, core_to):
        return {"qrow": y_to * 2 + core_to, "kcol": c_to}

    def held(w, s):
        return kv[w].at[pl.ds(s * kb, kb)]

    def remote(src, dst, send, recv, where):
        return pltpu.make_async_remote_copy(
            src_ref=src, dst_ref=dst, send_sem=send, recv_sem=recv,
            device_id=where, device_id_type=MESH,
        )

    core_peer = at(c, y, other)
    has_left, has_right = c > 0, c < nk - 1
    left, right = at(c - 1, y, core), at(c + 1, y, core)
    own = shard(c, y, core)
    barrier = pltpu.get_barrier_semaphore()

    def greet(where):
        pl.semaphore_signal(barrier, inc=1, device_id=where, device_id_type=MESH)

    pl.when(has_left)(lambda: greet(left))
    pl.when(has_right)(lambda: greet(right))
    for e in range(1, ny):
        greet(at(c, why(e), core))
    greet(core_peer)
    loads[0].wait()
    loads[1].wait()
    line_peers = (c + nk - 1) // nk + (2 * nk - 2 - c) // nk
    pl.semaphore_wait(barrier, line_peers + ny)

    y_sends = nk * (ny - 1)
    y_base = 2 * nk
    core_base = y_base + y_sends

    def gather(w, slot, s, where):
        return remote(held(w, s), held(w, s), ag_send.at[w, slot], ag_recv.at[w, s], where)

    def arrived(w, s):
        gather(w, 0, s, core_peer).wait_recv()

    def go_right(w, c_at):
        pl.when(has_right)(lambda: gather(w, c_at, shard(c_at, y, core), right).start())

    def go_left(w, c_at):
        pl.when(has_left)(lambda: gather(w, nk + c_at, shard(c_at, y, core), left).start())

    def go_y(w, c_at):
        for e in range(1, ny):
            slot = y_base + (e - 1) * nk + c_at
            gather(w, slot, shard(c_at, y, core), at(c, why(e), core)).start()

    def go_core(w, c_at, y_at):
        gather(w, core_base + y_at * nk + c_at, shard(c_at, y_at, core), core_peer).start()

    def along_z(w, i):
        @pl.when(c - i >= 0)
        def _():
            arrived(w, shard(c - i, y, core))
            go_right(w, c - i)
            go_y(w, c - i)
            go_core(w, c - i, y)

        @pl.when(c + i < nk)
        def _():
            arrived(w, shard(c + i, y, core))
            go_left(w, c + i)
            go_y(w, c + i)
            go_core(w, c + i, y)

    def along_y(w, i):
        def take(c_at, e):
            arrived(w, shard(c_at, why(e), core))
            go_core(w, c_at, why(e))

        def each(e, carry):
            pl.when(c - i >= 0)(lambda: take(c - i, e))
            if i:
                pl.when(c + i < nk)(lambda: take(c + i, e))
            return carry

        lax.fori_loop(1, ny, each, 0)

    def from_core(w):
        def each(i, carry):
            arrived(w, shard(i % nk, i // nk, other))
            return carry

        lax.fori_loop(0, nk * ny, each, 0)

    def gathers_sent(w):
        def each(c_at, carry):
            pl.when(has_right & (c_at <= c))(lambda: gather(w, c_at, own, right).wait_send())
            pl.when(has_left & (c_at >= c))(lambda: gather(w, nk + c_at, own, left).wait_send())
            return carry

        def rest(i, carry):
            gather(w, y_base + i, own, core_peer).wait_send()
            return carry

        lax.fori_loop(0, nk, each, 0)
        lax.fori_loop(0, y_sends + nk * ny, rest, 0)

    first_row = (r * nk + c) * qb
    zero_slot = qb * nnz
    parts = [slice(n * BLK, n * BLK + rows) for n in range(0, nnz, chunk)]

    def prepare():
        loads[2].wait()
        loads[3].wait()
        for b in range(qb):
            for h in range(H):
                q_h = q_ref[b * BLK : (b + 1) * BLK, h * HD : (h + 1) * HD]
                g_h = g_ref[b * BLK : (b + 1) * BLK, h * HD : (h + 1) * HD]
                qs[b, h * BLK : (h + 1) * BLK, :] = q_h
                gs[b, h * BLK : (h + 1) * BLK, :] = g_h
                qt[b, :, h * BLK : (h + 1) * BLK] = q_h.T
                gt[b, :, h * BLK : (h + 1) * BLK] = g_h.T
        slots[KEY, zero_slot] = jnp.zeros((BLK, HD), F32)
        slots[VALUE, zero_slot] = jnp.zeros((BLK, HD), F32)
        nothing = jnp.zeros(z_in.shape[2:], BF16)

        @pl.when(c == 0)
        def _():
            for w in range(2):
                z_in[w, 0] = nothing

        @pl.when(c == nk - 1)
        def _():
            for w in range(2):
                z_in[w, 1] = nothing

    def invert(j, carry):
        for b in range(qb):
            found = jnp.int32(zero_slot)
            for n in range(nnz):
                found = jnp.where(pat_ref[n, first_row + b] == j, b * nnz + n, found)
            inv[b, j] = found
        return carry

    def pick(w, scr, b):
        for n in range(nnz):
            scr[b, n * BLK : (n + 1) * BLK, :] = kv[w][pat_ref[n, first_row + b]]

    def score(b):
        pick(KEY, kc_scr, b)
        top = None
        for part in parts:
            scores = dot(kc_scr[b, part, :], qt[b])
            s_scr[b, part, :] = scores
            high = jnp.max(scores, axis=0, keepdims=True)
            top = high if top is None else jnp.maximum(top, high)
        return top

    def forward(b, top):
        total = jnp.zeros((1, H * BLK), F32)
        mix = jnp.zeros((HD, H * BLK), F32)
        for part in parts:
            weights = jnp.exp2((s_scr[b, part, :] - top) * (scaling * math.log2(math.e)))
            s_scr[b, part, :] = weights
            total = total + jnp.sum(weights, axis=0, keepdims=True)
            mix = mix + dot_t(vc_scr[b, part, :], weights.astype(BF16))
        attended = (mix / total).astype(BF16)
        delta = jnp.sum(gt[b].astype(F32) * attended.astype(F32), axis=0, keepdims=True)
        share = 1.0 / total
        for h in range(H):
            o_ref[b * BLK : (b + 1) * BLK, h * HD : (h + 1) * HD] = attended[
                :, h * BLK : (h + 1) * BLK
            ].T
        for n, part in enumerate(parts):
            prob = s_scr[b, part, :] * share
            s_scr[b, part, :] = prob
            grad_v = dot(prob.astype(BF16), gs[b])
            for i in range(chunk):
                slots[VALUE, b * nnz + n * chunk + i] = grad_v[i * BLK : (i + 1) * BLK]
        return delta

    def backward(b, delta):
        grad_q = jnp.zeros((HD, H * BLK), F32)
        for n, part in enumerate(parts):
            grad_prob = dot(vc_scr[b, part, :], gt[b])
            grad_score = (s_scr[b, part, :] * (grad_prob - delta)).astype(BF16)
            grad_k = dot(grad_score, qs[b]) * scaling
            grad_q = grad_q + dot_t(kc_scr[b, part, :], grad_score)
            for i in range(chunk):
                slots[KEY, b * nnz + n * chunk + i] = grad_k[i * BLK : (i + 1) * BLK]
        grad_q = (grad_q * scaling).astype(BF16)
        for h in range(H):
            dq_ref[b * BLK : (b + 1) * BLK, h * HD : (h + 1) * HD] = grad_q[
                :, h * BLK : (h + 1) * BLK
            ].T

    def partial(w, s, half):
        j = s * kb + half
        value = slots[w, inv[0, j]]
        for b in range(1, qb):
            value = value + slots[w, inv[b, j]]
        return value

    def to_core(w, i, s):
        return remote(
            held(w, s), core_in.at[w, i], core_send.at[w, i], core_recv.at[w, i], core_peer
        )

    def to_y(w, i, s, where):
        return remote(held(w, s), y_in.at[w, i], y_send.at[w, i], y_recv.at[w, i], where)

    def to_z(w, side, i, s, where):
        return remote(
            held(w, s), z_in.at[w, side, i], z_send.at[w, side, i], z_recv.at[w, side, i], where
        )

    def core_stage(w):
        def each(i, carry):
            c_at, y_at = (c + nk // 2 + i) % nk, (y + 1 + i // nk) % ny
            s = shard(c_at, y_at, other)
            for half in range(kb):
                kv[w][s * kb + half] = partial(w, s, half).astype(BF16)
            to_core(w, y_at * nk + c_at, s).start()
            return carry

        lax.fori_loop(0, nk * ny, each, 0)

    def y_stage(w):
        def one(c_at, e):
            y_at = why(e)
            s = shard(c_at, y_at, core)
            i = y_at * nk + c_at
            to_core(w, i, s).wait_recv()
            for half in range(kb):
                value = partial(w, s, half) + core_in[w, i, half].astype(F32)
                kv[w][s * kb + half] = value.astype(BF16)
            to_y(w, (e - 1) * nk + c_at, s, at(c, y_at, core)).start()

        def each(e, carry):
            for i in range(nk - 1, 0, -1):
                pl.when(c + i < nk)(lambda i=i: one(c + i, e))
                pl.when(c - i >= 0)(lambda i=i: one(c - i, e))
            one(c, e)
            return carry

        lax.fori_loop(1, ny, each, 0)

    def landed(w, c_at):
        to_core(w, y * nk + c_at, own).wait_recv()
        for e in range(1, ny):
            to_y(w, (e - 1) * nk + c_at, own, core_peer).wait_recv()

    def summed(w, c_at, half):
        value = partial(w, shard(c_at, y, core), half)
        value = value + core_in[w, y * nk + c_at, half].astype(F32)
        for e in range(1, ny):
            value = value + y_in[w, (e - 1) * nk + c_at, half].astype(F32)
        return value

    def z_stage(w):
        def one(c_at, side, has_source, where):
            landed(w, c_at)
            s = shard(c_at, y, core)
            pl.when(has_source)(lambda: to_z(w, side, c_at, own, where).wait_recv())
            for half in range(kb):
                value = summed(w, c_at, half) + z_in[w, side, c_at, half].astype(F32)
                kv[w][s * kb + half] = value.astype(BF16)
            to_z(w, side, c_at, s, where).start()

        for i in range(nk - 1, 0, -1):
            pl.when(c + i < nk)(lambda i=i: one(c + i, 0, has_left, right))
            pl.when(c - i >= 0)(lambda i=i: one(c - i, 1, has_right, left))

    def finish(w, out):
        landed(w, c)
        pl.when(has_left)(lambda: to_z(w, 0, c, own, core_peer).wait_recv())
        pl.when(has_right)(lambda: to_z(w, 1, c, own, core_peer).wait_recv())
        for half in range(kb):
            value = summed(w, c, half)
            for side in range(2):
                value = value + z_in[w, side, c, half].astype(F32)
            out[half] = value.astype(BF16)

    def sums_sent(w):
        def core_sent(i, carry):
            to_core(w, i, own).wait_send()
            return carry

        def y_sent(i, carry):
            to_y(w, i, own, core_peer).wait_send()
            return carry

        def z_sent(i, carry):
            pl.when(i > c)(lambda: to_z(w, 0, i, own, core_peer).wait_send())
            pl.when(i < c)(lambda: to_z(w, 1, i, own, core_peer).wait_send())
            return carry

        lax.fori_loop(0, nk * ny, core_sent, 0)
        lax.fori_loop(0, y_sends, y_sent, 0)
        lax.fori_loop(0, nk, z_sent, 0)

    go_right(KEY, c)
    go_left(KEY, c)
    go_y(KEY, c)
    go_y(VALUE, c)
    go_core(KEY, c, y)
    go_core(VALUE, c, y)
    prepare()
    for i in range(1, nk):
        along_z(KEY, i)
        if i == 1:
            go_right(VALUE, c)
            go_left(VALUE, c)
            lax.fori_loop(0, key_blocks, invert, 0)
        along_y(KEY, i - 1)
        if i > 1:
            along_z(VALUE, i - 1)
        if i > 2:
            along_y(VALUE, i - 3)
    along_y(KEY, nk - 1)
    along_z(VALUE, nk - 1)
    for i in range(max(nk - 3, 0), nk - 1):
        along_y(VALUE, i)
    from_core(KEY)
    tops = [score(b) for b in range(qb)]
    along_y(VALUE, nk - 1)
    from_core(VALUE)
    for b in range(qb):
        pick(VALUE, vc_scr, b)
    deltas = [forward(b, tops[b]) for b in range(qb)]
    gathers_sent(VALUE)
    core_stage(VALUE)
    backward(0, deltas[0])
    y_stage(VALUE)
    for b in range(1, qb):
        backward(b, deltas[b])
    gathers_sent(KEY)
    core_stage(KEY)
    z_stage(VALUE)
    y_stage(KEY)
    finish(VALUE, dv_ref)
    z_stage(KEY)
    finish(KEY, dk_ref)
    sums_sent(VALUE)
    sums_sent(KEY)


def vmem_bytes(scratch, blocks):
    held = sum(
        math.prod(piece.shape) * jnp.dtype(piece.dtype).itemsize
        for piece in scratch
        if piece.dtype in (F32, BF16)
    )
    return min(held + 2 * blocks + (4 << 20), 60 << 20)


def body(nq, nk, queries, keys, values, out_grad, pattern):
    nnz = pattern.shape[1]
    ny = nq // 2
    qb = queries.shape[0] // BLK
    kb = keys.shape[0] // BLK
    shards = nq * nk
    block = (kb, BLK, HD)
    y_sends = nk * (ny - 1)
    dma = pltpu.SemaphoreType.DMA
    vmem = pl.BlockSpec(memory_space=pltpu.VMEM)
    hbm = pl.BlockSpec(memory_space=pltpu.HBM)
    scratch = [
        pltpu.VMEM((shards * kb, BLK, HD), BF16),
        pltpu.VMEM((shards * kb, BLK, HD), BF16),
        pltpu.VMEM((2, nk * ny) + block, BF16),
        pltpu.VMEM((2, max(y_sends, 1)) + block, BF16),
        pltpu.VMEM((2, 2, nk) + block, BF16),
        pltpu.VMEM((2, qb * nnz + 1, BLK, HD), F32),
        pltpu.VMEM((qb, nnz * BLK, H * BLK), F32),
        pltpu.VMEM(queries.shape, BF16),
        pltpu.VMEM(queries.shape, BF16),
        pltpu.VMEM((qb, H * BLK, HD), BF16),
        pltpu.VMEM((qb, H * BLK, HD), BF16),
        pltpu.VMEM((qb, HD, H * BLK), BF16),
        pltpu.VMEM((qb, HD, H * BLK), BF16),
        pltpu.VMEM((qb, nnz * BLK, HD), BF16),
        pltpu.VMEM((qb, nnz * BLK, HD), BF16),
        pltpu.SMEM((qb, shards * kb), jnp.int32),
        dma((4,)),
        dma((2, 2 * nk + y_sends + nk * ny)),
        dma((2, shards)),
        dma((2, nk * ny)),
        dma((2, nk * ny)),
        dma((2, max(y_sends, 1))),
        dma((2, max(y_sends, 1))),
        dma((2, 2, nk)),
        dma((2, 2, nk)),
    ]
    attended, grad_q, grad_k, grad_v = pl.pallas_call(
        functools.partial(kernel, nq, nk, nnz),
        out_shape=(
            jax.ShapeDtypeStruct(queries.shape, BF16),
            jax.ShapeDtypeStruct(queries.shape, BF16),
            jax.ShapeDtypeStruct(block, BF16),
            jax.ShapeDtypeStruct(block, BF16),
        ),
        in_specs=[hbm] * 4 + [pl.BlockSpec(memory_space=pltpu.SMEM)],
        out_specs=(vmem,) * 4,
        scratch_shapes=scratch,
        compiler_params=pltpu.CompilerParams(
            collective_id=0,
            has_side_effects=True,
            vmem_limit_bytes=vmem_bytes(scratch, 4 * (queries.size + keys.size)),
        ),
    )(queries, out_grad, keys.reshape(block), values.reshape(block), pattern.T)
    return attended, grad_q, grad_k.reshape(keys.shape), grad_v.reshape(keys.shape)


def solution(mesh):
    return jax.shard_map(
        functools.partial(body, mesh.shape["qrow"], mesh.shape["kcol"]),
        mesh=mesh,
        in_specs=(
            P(("groups", "qrow", "kcol"), None),
            P(("groups", "kcol", "qrow"), None),
            P(("groups", "kcol", "qrow"), None),
            P(("groups", "qrow", "kcol"), None),
            P("groups", None),
        ),
        out_specs=(
            P(("groups", "qrow", "kcol"), None),
            P(("groups", "qrow", "kcol"), None),
            P(("groups", "kcol", "qrow"), None),
            P(("groups", "kcol", "qrow"), None),
        ),
        check_vma=False,
    )
```

```python
import functools
import math

import jax
import jax.numpy as jnp
from jax import lax
from jax.experimental import pallas as pl
from jax.experimental.pallas import tpu as pltpu
from jax.sharding import PartitionSpec as P

H = 4
HD = 128
BLK = 128
MESH = pl.DeviceIdType.MESH
F32 = jnp.float32
BF16 = jnp.bfloat16


def dot(a, b):
    return jnp.dot(a, b, preferred_element_type=F32)


def dot_t(a, b):
    return lax.dot_general(a, b, (((0,), (0,)), ((), ())), preferred_element_type=F32)


def kernel(
    nq, nk, nnz, q_hbm, g_hbm, k_hbm, v_hbm, pat_ref, o_ref, dq_ref, dk_ref, dv_ref,
    q_ref, g_ref, load_sem, kv, core_in, y_in, z_in, slots, s_scr, qs, gs, qt, gt, kc_scr, vc_scr, inv,
    ag_send, ag_recv, core_send, core_recv, y_send, y_recv, z_send, z_recv,
):
    ny = nq // 2
    qb = q_ref.shape[0] // BLK
    kb = k_hbm.shape[0]
    key_blocks = nq * nk * kb
    chunk = 2 if nnz % 2 == 0 else 1
    scaling = HD ** (-0.5)
    r = lax.axis_index("qrow")
    c = lax.axis_index("kcol")
    y, core = r // 2, r % 2
    other = 1 - core

    def shard(c_at, y_at, core_at):
        return c_at * nq + y_at * 2 + core_at

    def zed(d):
        return (c + d) % nk

    def why(e):
        return (y + e) % ny

    def at(c_to, y_to, core_to):
        return {"qrow": y_to * 2 + core_to, "kcol": c_to}

    def remote(src, dst, send, recv, where):
        return pltpu.make_async_remote_copy(
            src_ref=src, dst_ref=dst, send_sem=send, recv_sem=recv,
            device_id=where, device_id_type=MESH,
        )

    core_peer = at(c, y, other)
    own = shard(c, y, core)
    loads = [
        pltpu.make_async_copy(src, dst, load_sem.at[i])
        for i, (src, dst) in enumerate(
            ((k_hbm, kv.at[own, 0]), (v_hbm, kv.at[own, 1]), (q_hbm, q_ref), (g_hbm, g_ref))
        )
    ]
    for load in loads:
        load.start()

    barrier = pltpu.get_barrier_semaphore()
    for d in range(1, nk):
        pl.semaphore_signal(barrier, inc=1, device_id=at(zed(d), y, core), device_id_type=MESH)
    for e in range(1, ny):
        pl.semaphore_signal(barrier, inc=1, device_id=at(c, why(e), core), device_id_type=MESH)
    pl.semaphore_signal(barrier, inc=1, device_id=core_peer, device_id_type=MESH)

    loads[0].wait()
    loads[1].wait()
    pl.semaphore_wait(barrier, nk - 1 + ny - 1 + 1)

    z_sends = nk - 1
    y_sends = nk * (ny - 1)

    def gather(slot, s, where):
        return remote(kv.at[s], kv.at[s], ag_send.at[slot], ag_recv.at[s], where)

    def arrived(s):
        gather(0, s, core_peer).wait_recv()

    for d in range(1, nk):
        gather(d - 1, own, at(zed(d), y, core)).start()
    for e in range(1, ny):
        gather(z_sends + e - 1, own, at(c, why(e), core)).start()
    gather(z_sends + y_sends, own, core_peer).start()

    loads[2].wait()
    loads[3].wait()
    for b in range(qb):
        for h in range(H):
            q_h = q_ref[b * BLK : (b + 1) * BLK, h * HD : (h + 1) * HD]
            g_h = g_ref[b * BLK : (b + 1) * BLK, h * HD : (h + 1) * HD]
            qs[b, h * BLK : (h + 1) * BLK, :] = q_h
            gs[b, h * BLK : (h + 1) * BLK, :] = g_h
            qt[b, :, h * BLK : (h + 1) * BLK] = q_h.T
            gt[b, :, h * BLK : (h + 1) * BLK] = g_h.T

    zero_slot = qb * nnz
    slots[0, zero_slot] = jnp.zeros((BLK, HD), F32)
    slots[1, zero_slot] = jnp.zeros((BLK, HD), F32)
    first_row = (r * nk + c) * qb

    for d in range(1, nk):
        s = shard(zed(nk - d), y, core)
        arrived(s)
        for e in range(1, ny):
            gather(z_sends + d * (ny - 1) + e - 1, s, at(c, why(e), core)).start()
        gather(z_sends + y_sends + d, s, core_peer).start()

    def invert(j, carry):
        for b in range(qb):
            found = jnp.int32(zero_slot)
            for n in range(nnz):
                found = jnp.where(pat_ref[n, first_row + b] == j, b * nnz + n, found)
            inv[b, j] = found
        return carry

    lax.fori_loop(0, key_blocks, invert, 0)

    def from_y(i, carry):
        e, d = i // nk + 1, i % nk
        s = shard(zed(nk - d), why(ny - e), core)
        arrived(s)
        gather(z_sends + y_sends + nk + i, s, core_peer).start()
        return carry

    lax.fori_loop(0, y_sends, from_y, 0)

    def from_core(i, carry):
        arrived(shard(i % nk, i // nk, other))
        return carry

    lax.fori_loop(0, nk * ny, from_core, 0)

    rows = chunk * BLK
    for b in range(qb):
        for n in range(nnz):
            j = pat_ref[n, first_row + b]
            kc_scr[b, n * BLK : (n + 1) * BLK, :] = kv[j // kb, 0, j % kb]
            vc_scr[b, n * BLK : (n + 1) * BLK, :] = kv[j // kb, 1, j % kb]
    for b in range(qb):
        top = None
        for n in range(0, nnz, chunk):
            part = slice(n * BLK, n * BLK + rows)
            scores = dot(kc_scr[b, part, :], qt[b])
            s_scr[b, part, :] = scores
            high = jnp.max(scores, axis=0, keepdims=True)
            top = high if top is None else jnp.maximum(top, high)
        total = jnp.zeros((1, H * BLK), F32)
        mix = jnp.zeros((HD, H * BLK), F32)
        for n in range(0, nnz, chunk):
            part = slice(n * BLK, n * BLK + rows)
            weights = jnp.exp2((s_scr[b, part, :] - top) * (scaling * math.log2(math.e)))
            s_scr[b, part, :] = weights
            total = total + jnp.sum(weights, axis=0, keepdims=True)
            mix = mix + dot_t(vc_scr[b, part, :], weights.astype(BF16))
        attended = (mix / total).astype(BF16)
        delta = jnp.sum(gt[b].astype(F32) * attended.astype(F32), axis=0, keepdims=True)
        share = 1.0 / total
        for h in range(H):
            o_ref[b * BLK : (b + 1) * BLK, h * HD : (h + 1) * HD] = attended[
                :, h * BLK : (h + 1) * BLK
            ].T
        grad_q = jnp.zeros((HD, H * BLK), F32)
        for n in range(0, nnz, chunk):
            part = slice(n * BLK, n * BLK + rows)
            grad_prob = dot(vc_scr[b, part, :], gt[b])
            prob = s_scr[b, part, :] * share
            grad_score = (prob * (grad_prob - delta)).astype(BF16)
            grad_v = dot(prob.astype(BF16), gs[b])
            grad_k = dot(grad_score, qs[b]) * scaling
            grad_q = grad_q + dot_t(kc_scr[b, part, :], grad_score)
            for i in range(chunk):
                slots[0, b * nnz + n + i] = grad_k[i * BLK : (i + 1) * BLK]
                slots[1, b * nnz + n + i] = grad_v[i * BLK : (i + 1) * BLK]
        grad_q = (grad_q * scaling).astype(BF16)
        for h in range(H):
            dq_ref[b * BLK : (b + 1) * BLK, h * HD : (h + 1) * HD] = grad_q[
                :, h * BLK : (h + 1) * BLK
            ].T

    def gathers_sent(i, carry):
        gather(i, own, core_peer).wait_send()
        return carry

    lax.fori_loop(0, z_sends + y_sends + nk * ny, gathers_sent, 0)

    def partial(s, which, half):
        j = s * kb + half
        value = slots[which, inv[0, j]]
        for b in range(1, qb):
            value = value + slots[which, inv[b, j]]
        return value

    def to_core(i, s):
        return remote(kv.at[s], core_in.at[i], core_send.at[i], core_recv.at[i], core_peer)

    def to_y(i, s, c_at, where, slot):
        return remote(kv.at[s], y_in.at[i], y_send.at[slot], y_recv.at[i], where)

    def to_z(i, s, where):
        return remote(kv.at[s], z_in.at[i], z_send.at[i], z_recv.at[i], where)

    def order(i):
        return zed((i % nk + 1) % nk), why((i // nk + 1) % ny)

    def core_step(i, carry):
        c_at, y_at = order(i)
        s = shard(c_at, y_at, other)
        for which in range(2):
            for half in range(kb):
                kv[s, which, half] = partial(s, which, half).astype(BF16)
        to_core(i, s).start()
        return carry

    lax.fori_loop(0, nk * ny, core_step, 0)

    def y_step(i, carry):
        c_at, y_at = order(i)
        s = shard(c_at, y_at, core)
        to_core(i, s).wait_recv()
        for which in range(2):
            for half in range(kb):
                value = partial(s, which, half) + core_in[i, which, half].astype(F32)
                kv[s, which, half] = value.astype(BF16)
        to_y(i, s, c_at, at(c, y_at, core), i).start()
        return carry

    lax.fori_loop(0, y_sends, y_step, 0)

    def summed(d, s, which, half):
        i = y_sends + (d + nk - 1) % nk
        value = partial(s, which, half) + core_in[i, which, half].astype(F32)
        for e in range(1, ny):
            value = value + y_in[(e - 1) * nk + (d + nk - 1) % nk, which, half].astype(F32)
        return value

    def landed(d, s):
        to_core(y_sends + (d + nk - 1) % nk, s).wait_recv()
        for e in range(1, ny):
            to_y((e - 1) * nk + (d + nk - 1) % nk, s, c, core_peer, 0).wait_recv()

    for d in range(1, nk):
        s = shard(zed(d), y, core)
        landed(d, s)
        for which in range(2):
            for half in range(kb):
                kv[s, which, half] = summed(d, s, which, half).astype(BF16)
        to_z(d - 1, s, at(zed(d), y, core)).start()
    landed(0, own)
    for d in range(1, nk):
        to_z(d - 1, own, core_peer).wait_recv()
    for which, out in ((0, dk_ref), (1, dv_ref)):
        for half in range(kb):
            value = summed(0, own, which, half)
            for d in range(1, nk):
                value = value + z_in[d - 1, which, half].astype(F32)
            out[half] = value.astype(BF16)

    def core_sent(i, carry):
        to_core(i, own).wait_send()
        return carry

    def y_sent(i, carry):
        to_y(0, own, c, core_peer, i).wait_send()
        return carry

    lax.fori_loop(0, nk * ny, core_sent, 0)
    lax.fori_loop(0, y_sends, y_sent, 0)
    for d in range(1, nk):
        to_z(d - 1, own, core_peer).wait_send()


def vmem_bytes(scratch, blocks):
    held = sum(
        math.prod(piece.shape) * jnp.dtype(piece.dtype).itemsize
        for piece in scratch
        if piece.dtype in (F32, BF16)
    )
    return min(held + 2 * blocks + (4 << 20), 60 << 20)


def body(nq, nk, queries, keys, values, out_grad, pattern):
    nnz = pattern.shape[1]
    ny = nq // 2
    qb = queries.shape[0] // BLK
    kb = keys.shape[0] // BLK
    shards = nq * nk
    block = (2, kb, BLK, HD)
    tiles = (kb, BLK, HD)
    y_sends = nk * (ny - 1)
    dma = pltpu.SemaphoreType.DMA
    vmem = pl.BlockSpec(memory_space=pltpu.VMEM)
    scratch = [
        pltpu.VMEM(queries.shape, BF16),
        pltpu.VMEM(queries.shape, BF16),
        pltpu.SemaphoreType.DMA((4,)),
        pltpu.VMEM((shards,) + block, BF16),
        pltpu.VMEM((nk * ny,) + block, BF16),
        pltpu.VMEM((max(y_sends, 1),) + block, BF16),
        pltpu.VMEM((max(nk - 1, 1),) + block, BF16),
        pltpu.VMEM((2, qb * nnz + 1, BLK, HD), F32),
        pltpu.VMEM((qb, nnz * BLK, H * BLK), F32),
        pltpu.VMEM((qb, H * BLK, HD), BF16),
        pltpu.VMEM((qb, H * BLK, HD), BF16),
        pltpu.VMEM((qb, HD, H * BLK), BF16),
        pltpu.VMEM((qb, HD, H * BLK), BF16),
        pltpu.VMEM((qb, nnz * BLK, HD), BF16),
        pltpu.VMEM((qb, nnz * BLK, HD), BF16),
        pltpu.SMEM((qb, shards * kb), jnp.int32),
        dma((nk - 1 + y_sends + nk * ny,)),
        dma((shards,)),
        dma((nk * ny,)),
        dma((nk * ny,)),
        dma((max(y_sends, 1),)),
        dma((max(y_sends, 1),)),
        dma((max(nk - 1, 1),)),
        dma((max(nk - 1, 1),)),
    ]
    attended, grad_q, grad_k, grad_v = pl.pallas_call(
        functools.partial(kernel, nq, nk, nnz),
        out_shape=(
            jax.ShapeDtypeStruct(queries.shape, BF16),
            jax.ShapeDtypeStruct(queries.shape, BF16),
            jax.ShapeDtypeStruct(tiles, BF16),
            jax.ShapeDtypeStruct(tiles, BF16),
        ),
        in_specs=[pl.BlockSpec(memory_space=pltpu.HBM)] * 4 + [pl.BlockSpec(memory_space=pltpu.SMEM)],
        out_specs=(vmem,) * 4,
        scratch_shapes=scratch,
        compiler_params=pltpu.CompilerParams(
            collective_id=0, has_side_effects=True, vmem_limit_bytes=vmem_bytes(scratch, 4 * (queries.size + keys.size))
        ),
    )(queries, out_grad, keys.reshape(tiles), values.reshape(tiles), pattern.T)
    return attended, grad_q, grad_k.reshape(keys.shape), grad_v.reshape(keys.shape)


def solution(mesh):
    return jax.shard_map(
        functools.partial(body, mesh.shape["qrow"], mesh.shape["kcol"]),
        mesh=mesh,
        in_specs=(
            P(("groups", "qrow", "kcol"), None),
            P(("groups", "kcol", "qrow"), None),
            P(("groups", "kcol", "qrow"), None),
            P(("groups", "qrow", "kcol"), None),
            P("groups", None),
        ),
        out_specs=(
            P(("groups", "qrow", "kcol"), None),
            P(("groups", "qrow", "kcol"), None),
            P(("groups", "kcol", "qrow"), None),
            P(("groups", "kcol", "qrow"), None),
        ),
        check_vma=False,
    )
```
